32 devices in a mesh: groups: 2 (over x), blk: 8 (over z, y), rhs: 2 (over core).
Axes of the slice: x: 2, y: 2, z: 4, core: 2. Of those that a mesh axis runs over, the one named last changes fastest.
Arguments:
- factor: float32 [4, 8, 512, 2560], P('groups', 'blk'), parts along dimension 0, as said below
- rhs_blocks: float32 [4, 8, 512, 1024], P('groups', 'blk', None, 'rhs'), parts along dimension 0
Outputs:
- solved: float32 [4, 8, 512, 1024], P('groups', 'blk', None, 'rhs'), parts along dimension 0
- rest_rms: float32 [2, 1024], P('groups', 'rhs'), parts along dimension 0
There are 2 independent parts, one for each index of `groups`. The reference program is written for one: setup_inputs(seed, part) draws one part's arguments, and reference() takes and returns one part's arrays. A program takes and returns all parts, laid end to end along the dimension named above; each array names one. Nothing has to cross between parts.
Inputs may be any that keep to these rules, and one draw needn't show every extreme that they name: factor is zero above the diagonal of the whole factor, and its diagonal entries lie between 1 and 2.
All inputs are finite; a program needn't handle non-finite values.
Results may differ from the reference program's by a relative error of at most 0.0001.
Values sent between devices are 32-bit elements; how exact they have to be, the bound alone decides.
No kernel may reach another device: no remote copies, remote signals or barrier semaphores. Data moves between devices by JAX's collectives and lax.ppermute only.
A program may use at most 128 MiB of HBM per device.

```python
import math
import jax
import jax.numpy as jnp
from jax import lax

NB = 512
NRHS = 1024
BLK_DEV = 2
NBLOCKS = 16
COLS = 2560


def block_grid():
    per_index = NBLOCKS // BLK_DEV
    repeat_ids = jnp.arange(BLK_DEV, dtype=jnp.int32)[:, None, None, None]
    device_ids = jnp.arange(per_index, dtype=jnp.int32)[None, :, None, None]
    row_ids = jnp.arange(NB, dtype=jnp.int32)[None, None, :, None]
    return (repeat_ids * per_index + device_ids, row_ids, per_index)


def draw_factor(key, part):
    global_block, row_ids, per_index = block_grid()
    shape = (BLK_DEV, per_index, NB, COLS)
    col_ids = jnp.arange(COLS, dtype=jnp.int32)[None, None, None, :]
    col_block = col_ids // NB
    inner = col_ids % NB
    first, second, third = jax.random.split(key, 3)
    outside = jax.random.uniform(first, shape, jnp.float32, -1.0, 1.0) * (0.5 * math.sqrt(3.0) / math.sqrt(COLS))
    reach = 32.0
    strength = math.sqrt(1.0 - math.exp(-2.0 / reach))
    distance = jnp.maximum(row_ids - inner, 1).astype(jnp.float32)
    spread = jax.random.uniform(second, shape, jnp.float32, -math.sqrt(3.0), math.sqrt(3.0))
    within = spread * strength * jnp.exp(-(distance - 1.0) / reach)
    diagonal = jnp.exp(jax.random.uniform(third, shape, jnp.float32) * math.log(2.0))
    inblock = jnp.where(inner < row_ids, within, jnp.where(inner == row_ids, diagonal, 0.0))
    return jnp.where(col_block < global_block, outside, jnp.where(col_block == global_block, inblock, 0.0)).astype(jnp.float32)


def draw_rhs_blocks(key, part):
    global_block, row_ids, per_index = block_grid()
    shape = (BLK_DEV, per_index, NB, NRHS)
    first, second, third = jax.random.split(key, 3)
    position = (global_block * NB + row_ids).astype(jnp.float32) / (NBLOCKS * NB)
    row_factor = jnp.exp(jax.random.uniform(second, (BLK_DEV, per_index, NB, 1), jnp.float32) * math.log(3.3))
    col_factor = jnp.exp(jax.random.uniform(third, (1, 1, 1, NRHS), jnp.float32) * math.log(3.0))
    base = jax.random.normal(first, shape, jnp.float32)
    rising = 1.0 + 2.0 * position
    return (base * row_factor * col_factor * rising / 3.0).astype(jnp.float32)


def setup_inputs(seed: int = 0, part: int = 0) -> dict:
    key_of = jax.random.split(jax.random.key(seed), 3)
    own_keys = jax.random.split(jax.random.fold_in(key_of[2], part), 3)
    factor = draw_factor(jax.random.fold_in(jax.random.fold_in(key_of[2], part), 71), part)
    rhs_blocks = draw_rhs_blocks(jax.random.fold_in(jax.random.fold_in(key_of[2], part), 71), part)
    return {"factor": factor, "rhs_blocks": rhs_blocks}


def reference(factor, rhs_blocks):
    repeats, columns_dev, block_rows, panel_cols = factor.shape
    step_count = panel_cols // block_rows
    row_total = repeats * columns_dev * block_rows
    panel = factor.reshape(row_total, panel_cols)
    pending = rhs_blocks.reshape(row_total, rhs_blocks.shape[3])
    for step in range(step_count):
        offset = step * block_rows
        diagonal_block = jnp.tril(panel[offset:offset + block_rows, offset:offset + block_rows])
        block_solution = jax.scipy.linalg.solve_triangular(diagonal_block, pending[offset:offset + block_rows], lower=True)
        below = panel[offset + block_rows:, offset:offset + block_rows]
        update = jnp.dot(below.astype(jnp.float32), block_solution.astype(jnp.float32), precision=lax.Precision.HIGHEST, preferred_element_type=jnp.float32)
        pending = pending.at[offset + block_rows:].add(-update)
        pending = pending.at[offset:offset + block_rows].set(block_solution)
    remainder = pending[step_count * block_rows:]
    rest_rms = jnp.sqrt(lax.optimization_barrier(jnp.mean(remainder * remainder, axis=0)) + 1e-06)[None, :]
    return (pending.reshape(rhs_blocks.shape), rest_rms)
```

```python
import functools

import jax
import jax.numpy as jnp
from jax import lax
from jax.experimental import pallas as pl
from jax.experimental.pallas import tpu as pltpu
from jax.sharding import PartitionSpec as P


LANE = 128
BASE = 32
CHAIN = 3


def split(value):
    high = value.astype(jnp.bfloat16)
    return high, (value - high.astype(jnp.float32)).astype(jnp.bfloat16)


def dot_parts(ah, al, bh, bl):
    dot = functools.partial(jnp.dot, preferred_element_type=jnp.float32)
    return dot(ah, bh) + (dot(ah, bl) + dot(al, bh))


def dot3(a, b):
    return dot_parts(*split(a), *split(b))


def invert_lower(l_ref, inv_ref):
    n = l_ref.shape[0]
    tiles = BASE // 8
    rows = lax.broadcasted_iota(jnp.int32, (BASE, BASE), 0)
    cols = lax.broadcasted_iota(jnp.int32, (BASE, BASE), 1)
    inv_ref[...] = jnp.zeros((n, n), jnp.float32)
    for start in range(0, n, BASE):
        block = l_ref[start : start + BASE, start : start + BASE]
        diag = jnp.where(rows == cols, block, 0.0)
        across = 1.0 / jnp.sum(diag, axis=0, keepdims=True)
        down = 1.0 / jnp.sum(diag, axis=1, keepdims=True)
        unit = jnp.where(rows > cols, block * across, 0.0)
        eye = jnp.where(rows == cols, 1.0, 0.0).astype(jnp.float32)
        unit = [unit[8 * t : 8 * t + 8] for t in range(tiles)]
        out = [eye[8 * t : 8 * t + 8] for t in range(tiles)]
        for q in range(tiles):
            head = out[q]
            for s in range(7):
                head = head - unit[q][:, 8 * q + s : 8 * q + s + 1] * head[s : s + 1, :]
            out[q] = head
            for t in range(q + 1, tiles):
                tail = out[t]
                for s in range(8):
                    tail = tail - unit[t][:, 8 * q + s : 8 * q + s + 1] * head[s : s + 1, :]
                out[t] = tail
        inv_ref[start : start + BASE, start : start + BASE] = jnp.concatenate(out, axis=0) * down
    size = BASE
    while size < n:
        for o in range(0, n, 2 * size):
            top = inv_ref[o : o + size, o : o + size]
            bottom = inv_ref[o + size : o + 2 * size, o + size : o + 2 * size]
            cross = l_ref[o + size : o + 2 * size, o : o + size]
            inv_ref[o + size : o + 2 * size, o : o + size] = -dot3(bottom, dot3(cross, top))
        size *= 2


def first_kernel(steps, ids, l_ref, w_ref, inv_ref, *lanes):
    @pl.when(ids[0] < steps)
    def _():
        invert_lower(l_ref, inv_ref)
        solved = dot3(inv_ref[...], w_ref[...])
        for c, lane in enumerate(lanes):
            lane[...] = solved[:, c * LANE : (c + 1) * LANE]

    @pl.when(ids[0] >= steps)
    def _():
        inv_ref[...] = jnp.zeros(inv_ref.shape, jnp.float32)
        for c, lane in enumerate(lanes):
            lane[...] = w_ref[:, c * LANE : (c + 1) * LANE]


def prepare_kernel(steps, ids, f_ref, inv_ref, high_ref, low_ref):
    j = pl.program_id(0)
    device = ids[0]

    def put(row, value):
        high_ref[row], low_ref[row] = split(value)

    @pl.when(device >= steps)
    def _():
        put(0, f_ref[0])

    @pl.when(jnp.logical_and(device < steps, j < device))
    def _():
        put(0, dot3(inv_ref[...], f_ref[0]))

    @pl.when(jnp.logical_and(device < steps, j >= device))
    def _():
        put(0, jnp.zeros(inv_ref.shape, jnp.float32))

    for row in range(1, high_ref.shape[0]):
        put(row, f_ref[row])


def update_kernel(step, ids, high_ref, low_ref, mine_ref, other_ref, a_ref, b_ref, rest_ref, a_out, b_out, rest_out):
    owner = ids[0] == step
    even = ids[0] % 2 == 0
    mine, other = mine_ref[...], other_ref[...]
    left = jnp.where(owner, a_ref[...], jnp.where(even, mine, other))
    right = jnp.where(owner, b_ref[...], jnp.where(even, other, mine))
    xh, xl = split(jnp.concatenate([left, right], axis=1))
    change = dot_parts(high_ref[0], low_ref[0], xh, xl)
    a_out[...] = a_ref[...] - change[:, :LANE]
    b_out[...] = b_ref[...] - change[:, LANE:]
    for row in range(1, high_ref.shape[0]):
        rest_out[row - 1] = rest_ref[row - 1] - dot_parts(high_ref[row], low_ref[row], xh, xl)


def routes(count, step):
    planes = count // 2
    home = step // 2
    hops = []
    for sign, reach in ((1, planes - 1 - home), (-1, home)):
        previous = None
        for h in range(1, min(reach, CHAIN) + 1):
            hops.append((previous, [(home + sign * (h - 1), home + sign * h)]))
            previous = len(hops) - 1
        done = min(reach, CHAIN)
        while done < reach:
            moved = [(home + sign * (h - done), home + sign * h) for h in range(done + 1, min(reach, 2 * done) + 1)]
            hops.append(("all", moved))
            done = min(reach, 2 * done)
    return home, hops


def body(factor, rhs_blocks):
    repeats, _, rows, panel_cols = factor.shape
    width = rhs_blocks.shape[3]
    steps = panel_cols // rows
    count = lax.axis_size("blk")
    device = lax.axis_index("blk").astype(jnp.int32)
    plane, side = device // 2, device % 2
    ids = jnp.stack([device, jnp.minimum(device, steps - 1)])
    lanes = width // LANE
    f32 = jnp.float32

    square = jax.ShapeDtypeStruct((rows, rows), f32)
    lane_shape = jax.ShapeDtypeStruct((rows, LANE), f32)
    whole = lambda shape: pl.BlockSpec(shape, lambda *_: (0,) * len(shape))
    first = pl.pallas_call(
        functools.partial(first_kernel, steps),
        grid_spec=pltpu.PrefetchScalarGridSpec(
            num_scalar_prefetch=1,
            grid=(1,),
            in_specs=[
                pl.BlockSpec((None, None, rows, rows), lambda i, s: (0, 0, 0, s[1])),
                pl.BlockSpec((None, None, rows, width), lambda i, s: (0, 0, 0, 0)),
            ],
            out_specs=[whole((rows, rows))] + [whole((rows, LANE))] * lanes,
        ),
        out_shape=[square] + [lane_shape] * lanes,
        name="invert",
    )(ids, factor, rhs_blocks)
    inverse, top = first[0], list(first[1:])

    parts = jax.ShapeDtypeStruct((repeats, rows, panel_cols), jnp.bfloat16)
    high, low = pl.pallas_call(
        functools.partial(prepare_kernel, steps),
        grid_spec=pltpu.PrefetchScalarGridSpec(
            num_scalar_prefetch=1,
            grid=(steps,),
            in_specs=[
                pl.BlockSpec((repeats, None, rows, rows), lambda j, s: (0, 0, 0, j)),
                pl.BlockSpec((rows, rows), lambda j, s: (0, 0)),
            ],
            out_specs=[pl.BlockSpec((repeats, rows, rows), lambda j, s: (0, 0, j))] * 2,
        ),
        out_shape=[parts, parts],
        name="prepare",
    )(ids, factor, inverse)

    groups = lanes // 2
    pair = 2 * LANE
    rest = [rhs_blocks[1:, 0, :, g * pair : (g + 1) * pair] for g in range(groups)]
    rest_shape = jax.ShapeDtypeStruct((repeats - 1, rows, pair), f32)

    def update(step, mine, other, a, b, below):
        part = pl.BlockSpec((repeats, rows, rows), lambda i, s: (0, 0, step))
        lane = whole((rows, LANE))
        wide = whole((repeats - 1, rows, pair))
        return pl.pallas_call(
            functools.partial(update_kernel, step),
            grid_spec=pltpu.PrefetchScalarGridSpec(
                num_scalar_prefetch=1,
                grid=(1,),
                in_specs=[part, part, lane, lane, lane, lane, wide],
                out_specs=[lane, lane, wide],
            ),
            out_shape=[lane_shape, lane_shape, rest_shape],
            name="update",
        )(ids, high, low, mine, other, a, b, below)

    send = lambda value, pairs: lax.ppermute(value, "blk", pairs)
    both = lambda moves: [(2 * s + y, 2 * t + y) for s, t in moves for y in range(2)]

    for step in range(steps):
        home, hops = routes(count, step)
        yk = step % 2
        mate = step ^ 1
        for g in range(groups):
            pairs = (top[2 * g], top[2 * g + 1])
            across = send(pairs[1 - yk], [(step, mate)])
            straight = send(pairs[yk], [(step, mate)])
            start = jnp.where(device == step, pairs[yk], across)
            held = jnp.where(plane == home, start, 0)
            received = []
            near = None
            for source, moves in hops:
                payload = start if source is None else held if source == "all" else received[source]
                got = send(payload, both(moves))
                received.append(got)
                low_p = min(t for _, t in moves)
                high_p = max(t for _, t in moves)
                inside = (plane >= low_p) & (plane <= high_p)
                held = jnp.where(inside, got, held)
                if yk == 1 and moves == [(home, home + 1)]:
                    near = send(got, [(2 * home + 2, 2 * home + 3), (2 * home + 3, 2 * home + 2)])
            skip = {home} | ({home + 1} if near is not None else set())
            swap = [(2 * p + y, 2 * p + 1 - y) for p in range(count // 2) if p not in skip for y in range(2)]
            other = send(held, swap)
            other = jnp.where(plane == home, straight, other)
            if near is not None:
                other = jnp.where(plane == home + 1, near, other)
            top[2 * g], top[2 * g + 1], rest[g] = update(
                step, held, other, top[2 * g], top[2 * g + 1], rest[g]
            )

    keep = device >= steps
    first_row = jnp.concatenate(top, axis=1)
    below = jnp.concatenate(rest, axis=2)
    solved = jnp.concatenate([first_row[None], below], axis=0)
    squares = jnp.sum(below * below, axis=(0, 1)) + jnp.where(keep, jnp.sum(first_row * first_row, axis=0), 0.0)
    total = squares
    if count & (count - 1) == 0:
        distance = 1
        while distance < count:
            total = total + send(total, [(i, i ^ distance) for i in range(count)])
            distance *= 2
    else:
        total = lax.psum(squares, "blk")
    rest_count = (repeats * count - steps) * rows
    rest_rms = jnp.sqrt(total / rest_count + 1e-06)[None, :]
    return (solved[:, None], rest_rms)


def solution(mesh):
    placed = (P("groups", "blk", None, None), P("groups", "blk", None, "rhs"))
    return jax.shard_map(
        body,
        mesh=mesh,
        in_specs=placed,
        out_specs=(P("groups", "blk", None, "rhs"), P("groups", "rhs")),
        check_vma=False,
    )
```

```python
import functools

import jax
import jax.numpy as jnp
from jax import lax
from jax.experimental import pallas as pl
from jax.experimental.pallas import tpu as pltpu
from jax.sharding import PartitionSpec as P


GROUPS = 2
BASE = 32
CHAIN = 3
MIB = 1 << 20

ORDER = (
    "inv", "U10_0", "U10_1", "Y0_0", "prep3", "U20_0", "prep0", "X1_0_0", "Y0_1", "early1_0", "prep1", "U11_0",
    "C1_0", "early1_1", "U20_1", "X1_0_1", "X2_0_0", "U30_0", "C1_1", "prep2", "pre2_0", "U11_1", "pre2_1",
    "early2_0", "U12_0", "pre3_0", "Y2_0", "D12_0", "U21_0", "U30_1", "X2_0_1", "U21_1", "early2_1", "U12_1",
    "X2_1_0", "Y2_1", "U31_0", "pre3_1", "early3_0", "D12_1", "X3_0_0", "C3_0", "X3_0_1", "Y1_1", "U22_0", "early3_1",
    "U31_1", "X2_1_1", "Y1_0", "U13_0", "U22_1", "C3_1", "X0_2_0", "bulk0_0", "D13_1", "pre4_0", "early4_0", "D14_0",
    "X2_2_1", "Y3_0", "pre4_1", "U13_1", "X3_1_0", "X2_2_0", "D13_0", "early4_1", "D14_1", "U23_0", "U14_0", "prep4",
    "bulk0_1", "X3_2_0", "Y4_0", "D24_0", "X3_1_1", "X0_2_1", "bulk1_0", "U14_1", "X0_3_1", "U23_1", "D24_1",
    "X3_2_1", "X1_4_0", "bulk1_1", "Y3_1", "Y4_1", "X1_4_1", "X0_4_0", "X3_3_0", "X3_4_0", "X3_3_1", "X0_3_0",
    "bulk2_1", "bulk2_0", "X0_4_1", "X3_4_1", "bulk3_0", "bulk3_1", "bulk4_0", "bulk4_1",
)


def split(value):
    high = value.astype(jnp.bfloat16)
    return high, (value - high.astype(jnp.float32)).astype(jnp.bfloat16)


def dot_parts(ah, al, bh, bl):
    dot = functools.partial(jnp.dot, preferred_element_type=jnp.float32)
    return dot(ah, bh) + (dot(ah, bl) + dot(al, bh))


def dot3(a, b):
    return dot_parts(*split(a), *split(b))


def invert_lower(l_ref, inv_ref):
    n = l_ref.shape[0]
    tiles = BASE // 8
    rows = lax.broadcasted_iota(jnp.int32, (BASE, BASE), 0)
    cols = lax.broadcasted_iota(jnp.int32, (BASE, BASE), 1)
    inv_ref[...] = jnp.zeros((n, n), jnp.float32)
    for start in range(0, n, BASE):
        block = l_ref[start : start + BASE, start : start + BASE]
        diag = jnp.where(rows == cols, block, 0.0)
        across = 1.0 / jnp.sum(diag, axis=0, keepdims=True)
        down = 1.0 / jnp.sum(diag, axis=1, keepdims=True)
        unit = jnp.where(rows > cols, block * across, 0.0)
        eye = jnp.where(rows == cols, 1.0, 0.0).astype(jnp.float32)
        unit = [unit[8 * t : 8 * t + 8] for t in range(tiles)]
        out = [eye[8 * t : 8 * t + 8] for t in range(tiles)]
        for q in range(tiles):
            head = out[q]
            for s in range(7):
                head = head - unit[q][:, 8 * q + s : 8 * q + s + 1] * head[s : s + 1, :]
            out[q] = head
            for t in range(q + 1, tiles):
                tail = out[t]
                for s in range(8):
                    tail = tail - unit[t][:, 8 * q + s : 8 * q + s + 1] * head[s : s + 1, :]
                out[t] = tail
        inv_ref[start : start + BASE, start : start + BASE] = jnp.concatenate(out, axis=0) * down
    size = BASE
    while size < n:
        for o in range(0, n, 2 * size):
            top = inv_ref[o : o + size, o : o + size]
            bottom = inv_ref[o + size : o + 2 * size, o + size : o + 2 * size]
            cross = l_ref[o + size : o + 2 * size, o : o + size]
            inv_ref[o + size : o + 2 * size, o : o + size] = -dot3(bottom, dot3(cross, top))
        size *= 2


def invert_kernel(steps, ids, factor, rhs, inv_ref, *refs):
    tops, (l_ref, w_ref, sem) = refs[:-3], refs[-3:]
    device = ids[0]
    rows = l_ref.shape[0]
    column = pl.multiple_of(jnp.minimum(device, steps - 1) * rows, rows)
    copies = [
        pltpu.make_async_copy(factor.at[0, 0, :, pl.ds(column, rows)], l_ref, sem.at[0]),
        pltpu.make_async_copy(rhs.at[0, 0], w_ref, sem.at[1]),
    ]
    for copy in copies:
        copy.start()
    for copy in copies:
        copy.wait()

    @pl.when(device < steps)
    def _():
        invert_lower(l_ref, inv_ref)
        solved = dot3(inv_ref[...], w_ref[...])
        wide = tops[0].shape[1]
        for g, top in enumerate(tops):
            top[...] = solved[:, g * wide : (g + 1) * wide]


def prepare_kernel(steps, step, ids, factor, inv_ref, high_ref, low_ref, f_ref, sem):
    device = ids[0]
    rows = f_ref.shape[1]
    copy = pltpu.make_async_copy(factor.at[:, 0, :, pl.ds(step * rows, rows)], f_ref, sem)
    copy.start()
    copy.wait()

    def put(row, value):
        high_ref[row], low_ref[row] = split(value)

    @pl.when(device >= steps)
    def _():
        put(0, f_ref[0])

    @pl.when(jnp.logical_and(device < steps, device > step))
    def _():
        put(0, dot3(inv_ref[...], f_ref[0]))

    for row in range(1, f_ref.shape[0]):
        put(row, f_ref[row])


def solve_kernel(target, ids, base_ref, *refs):
    out = refs[-1]

    @pl.when(ids[0] == target)
    def _():
        value = base_ref[...]
        for i in range(0, len(refs) - 1, 3):
            high, low, x = refs[i : i + 3]
            value = value - dot_parts(high[0], low[0], *split(x[...]))
        out[...] = value


def rest_kernel(steps, step, last, ids, high, low, rest, *refs):
    if last:
        sources, (out, sums, xh, xl) = refs[:-4], refs[-4:]
    else:
        sources, (out, xh, xl) = refs[:-3], refs[-3:]
    for s, source in enumerate(sources):

        @pl.when(ids[1 + step] == s)
        def _():
            xh[...], xl[...] = split(source[...])

    def put(row):
        value = rest[row] - dot_parts(high[row], low[row], xh[...], xl[...])
        out[row] = value
        return jnp.sum(value * value, axis=0, keepdims=True)

    total = sum(put(row) for row in range(1, rest.shape[0]))
    if last:
        sums[...] = total

    @pl.when(ids[0] >= steps)
    def _():
        extra = put(0)
        if last:
            sums[...] = total + extra


def finish_kernel(steps, ids, *refs):
    out, sem = refs[-2:]
    groups = (len(refs) - 2) // (steps + 1)
    wide = out.shape[2] // groups

    def write(source, row, g):
        copy = pltpu.make_async_copy(source, out.at[row, :, pl.ds(g * wide, wide)], sem.at[row, g])
        copy.start()

    def settle(source, row, g):
        pltpu.make_async_copy(source, out.at[row, :, pl.ds(g * wide, wide)], sem.at[row, g]).wait()

    for go in (write, settle):
        for g in range(groups):
            mine, rest = refs[g * (steps + 1) : g * (steps + 1) + steps], refs[g * (steps + 1) + steps]
            for row in range(1, out.shape[0]):
                go(rest.at[row], row, g)
            for step in range(steps):

                @pl.when(ids[0] == step)
                def _():
                    go(mine[step], 0, g)

            @pl.when(ids[0] >= steps)
            def _():
                go(rest.at[0], 0, g)


class Op:
    def __init__(self, kind, deps, pairs=None, **info):
        self.kind, self.deps, self.pairs, self.info = kind, list(deps), pairs, info


def make_plan(count, steps, groups):
    planes = count // 2
    ops = {"inv": Op("inv", [])}
    source = {}
    for k in range(steps):
        home, y = divmod(k, 2)
        last = k == steps - 1
        ops[f"prep{k}"] = Op("prep", ["inv"], step=k)
        for g in range(groups):
            tag = f"{k}_{g}"
            own = "inv" if k == 0 else f"early{tag}"
            got = []

            def send(name, payload, pairs):
                name = name + tag
                ops[name] = Op("send", [payload], pairs, group=g)
                got.append(name)
                for _, b in pairs:
                    source[k, g, b] = name
                return name

            if y == 0:
                send("Y", own, [(k, k + 1)])
            elif not last:
                send("C", own, [(k, k + 1)])
            near = {}
            far = []
            for sign, reach, letter in ((1, planes - 1 - home, "U"), (-1, home, "D")):
                payload = own
                for h in range(1, min(reach, CHAIN) + 1):
                    a, b = home + sign * (h - 1), home + sign * h
                    payload = near[b] = send(f"{letter}{h}", payload, [(2 * a + y, 2 * b + y)])
                done = min(reach, CHAIN)
                while done < reach:
                    size = min(reach, 2 * done) - done
                    held = f"held{letter}{done}_{tag}"
                    ops[held] = Op("held", [own] + got, step=k, group=g, owner=k)
                    moved = [(home + sign * h, home + sign * (h + done)) for h in range(1, size + 1)]
                    send(f"{letter}{done + 1}", held, [(2 * a + y, 2 * b + y) for a, b in moved])
                    far += [b for _, b in moved]
                    done += size
            if y == 1:
                send("Y", own, [(k, k - 1)])
            for b, name in near.items():
                if not (y == 1 and not last and b == home + 1):
                    send(f"X{b}_", name, [(2 * b + y, 2 * b + 1 - y)])
            if far:
                held = f"held{tag}"
                ops[held] = Op("held", [own] + got, step=k, group=g, owner=k)
                send("F", held, [(2 * b + y, 2 * b + 1 - y) for b in far])
            if not last:
                base = "inv"
                if k > 0:
                    base = f"pre{k + 1}_{g}"
                    blocks = [(f"prep{j}", source[j, g, k + 1]) for j in range(k)]
                    ops[base] = Op("solve", ["inv"] + [n for b in blocks for n in b], device=k + 1, group=g)
                block = [f"prep{k}", source[k, g, k + 1]]
                ops[f"early{k + 1}_{g}"] = Op("solve", [base] + block, device=k + 1, group=g)
            before = [f"bulk{k - 1}_{g}"] if k else []
            ops[f"bulk{tag}"] = Op("rest", [f"prep{k}", own] + got + before, step=k, group=g, last=last)
    return ops


def arrange(ops, order):
    if set(order) != set(ops):
        order = list(ops)
    pending, placed, out = list(order), set(), []
    while pending:
        name = next(n for n in pending if all(d in placed for d in ops[n].deps))
        pending.remove(name)
        placed.add(name)
        out.append(name)
    return out


def body(order, ops, factor, rhs_blocks):
    repeats, _, rows, panel_cols = factor.shape
    width = rhs_blocks.shape[3]
    steps = panel_cols // rows
    count = lax.axis_size("blk")
    device = lax.axis_index("blk").astype(jnp.int32)
    groups = GROUPS
    wide = width // groups
    f32 = jnp.float32
    vmem = pl.BlockSpec(memory_space=pltpu.VMEM)
    smem = pl.BlockSpec(memory_space=pltpu.SMEM)
    hbm = pl.BlockSpec(memory_space=pl.ANY)
    shape = jax.ShapeDtypeStruct

    def call(kernel, ins, outs, specs=None, out_specs=None, scratch=(), limit=16, **more):
        return pl.pallas_call(
            kernel,
            out_shape=outs,
            in_specs=[smem] + (specs or [vmem] * len(ins)),
            out_specs=out_specs or [vmem] * len(outs),
            scratch_shapes=list(scratch),
            compiler_params=pltpu.CompilerParams(vmem_limit_bytes=limit * MIB),
            **more,
        )(ids, *ins)

    def origin(k, g):
        names = ops[f"bulk{k}_{g}"].deps[1:]
        table = [0] * count
        for s, name in enumerate(names):
            if ops[name].kind == "send":
                for _, b in ops[name].pairs:
                    table[b] = s
        return table

    tables = jnp.array([origin(k, 0) for k in range(steps)], jnp.int32)
    ids = jnp.concatenate([device[None], lax.dynamic_index_in_dim(tables, device, 1, keepdims=False)])

    square = shape((rows, rows), f32)
    chunk = shape((rows, wide), f32)
    parts = shape((repeats, rows, rows), jnp.bfloat16)
    below = shape((repeats, rows, wide), f32)
    env = {}
    tops = {}
    rest = {g: rhs_blocks[:, 0, :, g * wide : (g + 1) * wide] for g in range(groups)}
    sums = {}

    def own(name, g):
        return tops[g] if name == "inv" else env[name]

    def emit(name):
        op = ops[name]
        g = op.info.get("group")
        if op.kind == "inv":
            scratch = [pltpu.VMEM((rows, rows), f32), pltpu.VMEM((rows, width), f32), pltpu.SemaphoreType.DMA((2,))]
            got = call(
                functools.partial(invert_kernel, steps), [factor, rhs_blocks],
                [square] + [chunk] * groups, specs=[hbm, hbm], scratch=scratch,
            )
            env[name] = got[0]
            tops.update(enumerate(got[1:]))
        elif op.kind == "prep":
            scratch = [pltpu.VMEM((repeats, rows, rows), f32), pltpu.SemaphoreType.DMA]
            env[name] = call(
                functools.partial(prepare_kernel, steps, op.info["step"]), [factor, env["inv"]],
                [parts, parts], specs=[hbm, vmem], scratch=scratch,
            )
        elif op.kind == "send":
            env[name] = lax.ppermute(own(op.deps[0], g), "blk", op.pairs)
        elif op.kind == "held":
            value = own(op.deps[0], g)
            for other in op.deps[1:]:
                here = functools.reduce(jnp.logical_or, [device == b for _, b in ops[other].pairs])
                value = jnp.where(here, env[other], value)
            env[name] = value
        elif op.kind == "solve":
            ins = [own(op.deps[0], g)]
            for dep in op.deps[1:]:
                ins += env[dep] if ops[dep].kind == "prep" else [env[dep]]
            env[name] = call(functools.partial(solve_kernel, op.info["device"]), ins, [chunk])[0]
        else:
            k, last = op.info["step"], op.info["last"]
            names = [n for n in op.deps[1:] if ops[n].kind != "rest"]
            ins = list(env[op.deps[0]]) + [rest[g]] + [own(n, g) for n in names]
            outs = [below] + ([shape((1, wide), f32)] if last else [])
            scratch = [pltpu.VMEM((rows, wide), jnp.bfloat16)] * 2
            got = call(
                functools.partial(rest_kernel, steps, k, last), ins, outs, scratch=scratch,
                input_output_aliases={3: 0},
            )
            rest[g] = env[name] = got[0]
            if last:
                sums[g] = got[1]

    for name in order:
        emit(name)

    total = jnp.concatenate([sums[g] for g in range(groups)], axis=1)[0]
    send = lambda value, pairs: lax.ppermute(value, "blk", pairs)
    if count & (count - 1) == 0:
        distance = 1
        while distance < count:
            total = total + send(total, [(i, i ^ distance) for i in range(count)])
            distance *= 2
    else:
        total = lax.psum(total, "blk")
    rest_count = (repeats * count - steps) * rows
    rest_rms = jnp.sqrt(total / rest_count + 1e-06)[None, :]

    ins = []
    for g in range(groups):
        ins += [own("inv" if k == 0 else f"early{k}_{g}", g) for k in range(steps)] + [rest[g]]
    solved = call(
        functools.partial(finish_kernel, steps), ins, [shape((repeats, rows, width), f32)],
        out_specs=[hbm], scratch=[pltpu.SemaphoreType.DMA((repeats, groups))],
    )[0]
    return (solved[:, None], rest_rms)


def solution(mesh):
    placed = (P("groups", "blk", None, None), P("groups", "blk", None, "rhs"))
    count = mesh.shape["blk"]

    def whole(factor, rhs_blocks):
        steps = factor.shape[3] // factor.shape[2]
        ops = make_plan(count, steps, GROUPS)
        order = arrange(ops, ORDER)
        mapped = jax.shard_map(
            functools.partial(body, order, ops),
            mesh=mesh,
            in_specs=placed,
            out_specs=(P("groups", "blk", None, "rhs"), P("groups", "rhs")),
            check_vma=False,
        )
        return mapped(factor, rhs_blocks)

    return whole
```

```python
import functools

import jax
import jax.numpy as jnp
from jax import lax
from jax.experimental import pallas as pl
from jax.experimental.pallas import tpu as pltpu
from jax.sharding import PartitionSpec as P


GROUPS = 2
BASE = 32
CHAIN = 3
MIB = 1 << 20

ORDER = (
    "inv", "U10_0", "prep0", "Y0_0", "U10_1", "Y0_1", "U20_0", "X1_0_0", "early1_0", "pre2_0", "C1_0", "U11_0",
    "early1_1", "U20_1", "prep2", "prep1", "U21_0", "pre2_1", "U11_1", "U30_0", "early2_0", "Y2_0", "pre3_0", "U12_0",
    "C1_1", "X2_0_0", "prep4", "prep3", "X2_0_1", "D12_0", "U30_1", "U21_1", "X1_0_1", "U31_0", "X2_1_0", "early3_0",
    "C3_0", "early2_1", "X3_0_0", "Y2_1", "U22_0", "U12_1", "Y1_1", "U13_0", "X3_1_0", "bulk0_0", "X3_0_1", "U31_1",
    "pre4_0", "D13_0", "X0_2_0", "D12_1", "X2_1_1", "early4_0", "Y1_0", "pre3_1", "U14_0", "early3_1", "C3_1",
    "D14_0", "bulk0_1", "X0_2_1", "Y3_1", "X3_2_0", "X2_2_0", "U22_1", "X0_3_0", "U13_1", "X3_1_1", "pre4_1", "Y4_0",
    "U23_0", "D24_0", "early4_1", "D14_1", "bulk1_0", "X3_2_1", "bulk2_0", "U14_1", "U23_1", "bulk1_1", "D13_1",
    "X2_2_1", "Y3_0", "X0_4_0", "X3_3_0", "D24_1", "X1_4_0", "X3_4_0", "X3_4_1", "X3_3_1", "X1_4_1", "X0_3_1",
    "bulk3_0", "bulk4_0", "X0_4_1", "Y4_1", "bulk2_1", "bulk3_1", "bulk4_1",
)


def split(value):
    high = value.astype(jnp.bfloat16)
    return high, (value - high.astype(jnp.float32)).astype(jnp.bfloat16)


def dot_parts(ah, al, bh, bl):
    dot = functools.partial(jnp.dot, preferred_element_type=jnp.float32)
    return dot(ah, bh) + (dot(ah, bl) + dot(al, bh))


def dot3(a, b):
    return dot_parts(*split(a), *split(b))


def invert_lower(l_ref, inv_ref):
    n = l_ref.shape[0]
    tiles = BASE // 8
    rows = lax.broadcasted_iota(jnp.int32, (BASE, BASE), 0)
    cols = lax.broadcasted_iota(jnp.int32, (BASE, BASE), 1)
    inv_ref[...] = jnp.zeros((n, n), jnp.float32)
    for start in range(0, n, BASE):
        block = l_ref[start : start + BASE, start : start + BASE]
        diag = jnp.where(rows == cols, block, 0.0)
        across = 1.0 / jnp.sum(diag, axis=0, keepdims=True)
        down = 1.0 / jnp.sum(diag, axis=1, keepdims=True)
        unit = jnp.where(rows > cols, block * across, 0.0)
        eye = jnp.where(rows == cols, 1.0, 0.0).astype(jnp.float32)
        unit = [unit[8 * t : 8 * t + 8] for t in range(tiles)]
        out = [eye[8 * t : 8 * t + 8] for t in range(tiles)]
        for q in range(tiles):
            head = out[q]
            for s in range(7):
                head = head - unit[q][:, 8 * q + s : 8 * q + s + 1] * head[s : s + 1, :]
            out[q] = head
            for t in range(q + 1, tiles):
                tail = out[t]
                for s in range(8):
                    tail = tail - unit[t][:, 8 * q + s : 8 * q + s + 1] * head[s : s + 1, :]
                out[t] = tail
        inv_ref[start : start + BASE, start : start + BASE] = jnp.concatenate(out, axis=0) * down
    size = BASE
    while size < n:
        for o in range(0, n, 2 * size):
            top = inv_ref[o : o + size, o : o + size]
            bottom = inv_ref[o + size : o + 2 * size, o + size : o + 2 * size]
            cross = l_ref[o + size : o + 2 * size, o : o + size]
            inv_ref[o + size : o + 2 * size, o : o + size] = -dot3(bottom, dot3(cross, top))
        size *= 2


def invert_kernel(steps, ids, l_ref, w_ref, inv_ref, *tops):
    device = ids[0]

    @pl.when(device < steps)
    def _():
        invert_lower(l_ref, inv_ref)
        solved = dot3(inv_ref[...], w_ref[...])
        wide = tops[0].shape[1]
        for g, top in enumerate(tops):
            top[...] = solved[:, g * wide : (g + 1) * wide]


def prepare_kernel(steps, step, ids, factor, inv_ref, high_ref, low_ref, f_ref, sem):
    device = ids[0]
    rows = f_ref.shape[1]
    copy = pltpu.make_async_copy(factor.at[:, 0, :, pl.ds(step * rows, rows)], f_ref, sem)
    copy.start()
    copy.wait()

    def put(row, value):
        high_ref[row], low_ref[row] = split(value)

    @pl.when(device >= steps)
    def _():
        put(0, f_ref[0])

    @pl.when(jnp.logical_and(device < steps, device > step))
    def _():
        part = rows // 2

        def product(i, _):
            here = pl.ds(pl.multiple_of(i * part, part), part)
            high_ref[0, here], low_ref[0, here] = split(dot3(inv_ref[here, :], f_ref[0]))

        lax.fori_loop(0, 2, product, None)

    for row in range(1, f_ref.shape[0]):
        put(row, f_ref[row])


def solve_kernel(target, ids, base_ref, *refs):
    out = refs[-1]

    @pl.when(ids[0] == target)
    def _():
        value = base_ref[...]
        for i in range(0, len(refs) - 1, 3):
            high, low, x = refs[i : i + 3]
            value = value - dot_parts(high[0], low[0], *split(x[...]))
        out[...] = value


def rest_kernel(steps, step, last, ids, high, low, rest, *refs):
    if last:
        sources, (out, sums, xh, xl) = refs[:-4], refs[-4:]
    else:
        sources, (out, xh, xl) = refs[:-3], refs[-3:]
    for s, source in enumerate(sources):

        @pl.when(ids[1 + step] == s)
        def _():
            xh[...], xl[...] = split(source[...])

    def put(row, total):
        value = rest[row] - dot_parts(high[row], low[row], xh[...], xl[...])
        out[row] = value
        return total + jnp.sum(value * value, axis=0, keepdims=True) if last else total

    first = jnp.where(ids[0] >= steps, 0, 1)
    total = lax.fori_loop(first, rest.shape[0], put, jnp.zeros((1, xh.shape[1]), jnp.float32))
    if last:
        sums[...] = total


def finish_kernel(steps, ids, *refs):
    out, sem = refs[-2:]
    groups = (len(refs) - 2) // (steps + 1)
    wide = out.shape[2] // groups

    def write(source, row, g):
        copy = pltpu.make_async_copy(source, out.at[row, :, pl.ds(g * wide, wide)], sem.at[row, g])
        copy.start()

    def settle(source, row, g):
        pltpu.make_async_copy(source, out.at[row, :, pl.ds(g * wide, wide)], sem.at[row, g]).wait()

    for go in (write, settle):
        for g in range(groups):
            mine, rest = refs[g * (steps + 1) : g * (steps + 1) + steps], refs[g * (steps + 1) + steps]
            for row in range(1, out.shape[0]):
                go(rest.at[row], row, g)
            for step in range(steps):

                @pl.when(ids[0] == step)
                def _():
                    go(mine[step], 0, g)

            @pl.when(ids[0] >= steps)
            def _():
                go(rest.at[0], 0, g)


class Op:
    def __init__(self, kind, deps, pairs=None, **info):
        self.kind, self.deps, self.pairs, self.info = kind, list(deps), pairs, info


def make_plan(count, steps, groups):
    planes = count // 2
    ops = {"inv": Op("inv", [])}
    source = {}
    for k in range(steps):
        home, y = divmod(k, 2)
        last = k == steps - 1
        ops[f"prep{k}"] = Op("prep", ["inv"], step=k)
        for g in range(groups):
            tag = f"{k}_{g}"
            own = "inv" if k == 0 else f"early{tag}"
            got = []

            def send(name, payload, pairs):
                name = name + tag
                ops[name] = Op("send", [payload], pairs, group=g)
                got.append(name)
                for _, b in pairs:
                    source[k, g, b] = name
                return name

            if y == 0:
                send("Y", own, [(k, k + 1)])
            elif not last:
                send("C", own, [(k, k + 1)])
            near = {}
            far = []
            for sign, reach, letter in ((1, planes - 1 - home, "U"), (-1, home, "D")):
                payload = own
                for h in range(1, min(reach, CHAIN) + 1):
                    a, b = home + sign * (h - 1), home + sign * h
                    payload = near[b] = send(f"{letter}{h}", payload, [(2 * a + y, 2 * b + y)])
                done = min(reach, CHAIN)
                while done < reach:
                    size = min(reach, 2 * done) - done
                    held = f"held{letter}{done}_{tag}"
                    ops[held] = Op("held", [own] + got, step=k, group=g, owner=k)
                    moved = [(home + sign * h, home + sign * (h + done)) for h in range(1, size + 1)]
                    send(f"{letter}{done + 1}", held, [(2 * a + y, 2 * b + y) for a, b in moved])
                    far += [b for _, b in moved]
                    done += size
            if y == 1:
                send("Y", own, [(k, k - 1)])
            for b, name in near.items():
                if not (y == 1 and not last and b == home + 1):
                    send(f"X{b}_", name, [(2 * b + y, 2 * b + 1 - y)])
            if far:
                held = f"held{tag}"
                ops[held] = Op("held", [own] + got, step=k, group=g, owner=k)
                send("F", held, [(2 * b + y, 2 * b + 1 - y) for b in far])
            if not last:
                base = "inv"
                if k > 0:
                    base = f"pre{k + 1}_{g}"
                    blocks = [(f"prep{j}", source[j, g, k + 1]) for j in range(k)]
                    ops[base] = Op("solve", ["inv"] + [n for b in blocks for n in b], device=k + 1, group=g)
                block = [f"prep{k}", source[k, g, k + 1]]
                ops[f"early{k + 1}_{g}"] = Op("solve", [base] + block, device=k + 1, group=g)
            before = [f"bulk{k - 1}_{g}"] if k else []
            ops[f"bulk{tag}"] = Op("rest", [f"prep{k}", own] + got + before, step=k, group=g, last=last)
    return ops


def arrange(ops, order):
    if set(order) != set(ops):
        order = list(ops)
    pending, placed, out = list(order), set(), []
    while pending:
        name = next(n for n in pending if all(d in placed for d in ops[n].deps))
        pending.remove(name)
        placed.add(name)
        out.append(name)
    return out


def body(order, ops, factor, rhs_blocks):
    repeats, _, rows, panel_cols = factor.shape
    width = rhs_blocks.shape[3]
    steps = panel_cols // rows
    count = lax.axis_size("blk")
    device = lax.axis_index("blk").astype(jnp.int32)
    groups = GROUPS
    wide = width // groups
    f32 = jnp.float32
    vmem = pl.BlockSpec(memory_space=pltpu.VMEM)
    smem = pl.BlockSpec(memory_space=pltpu.SMEM)
    hbm = pl.BlockSpec(memory_space=pltpu.HBM)
    shape = jax.ShapeDtypeStruct

    def call(kernel, ins, outs, specs=None, out_specs=None, scratch=(), limit=16, **more):
        return pl.pallas_call(
            kernel,
            out_shape=outs,
            in_specs=[smem] + (specs or [vmem] * len(ins)),
            out_specs=out_specs or [vmem] * len(outs),
            scratch_shapes=list(scratch),
            compiler_params=pltpu.CompilerParams(vmem_limit_bytes=limit * MIB),
            **more,
        )(ids, *ins)

    def origin(k, g):
        names = ops[f"bulk{k}_{g}"].deps[1:]
        table = [0] * count
        for s, name in enumerate(names):
            if ops[name].kind == "send":
                for _, b in ops[name].pairs:
                    table[b] = s
        return table

    tables = jnp.array([origin(k, 0) for k in range(steps)], jnp.int32)
    ids = jnp.concatenate([device[None], lax.dynamic_index_in_dim(tables, device, 1, keepdims=False)])

    square = shape((rows, rows), f32)
    chunk = shape((rows, wide), f32)
    parts = shape((repeats, rows, rows), jnp.bfloat16)
    below = shape((repeats, rows, wide), f32)
    env = {}
    tops = {}
    rest = {g: rhs_blocks[:, 0, :, g * wide : (g + 1) * wide] for g in range(groups)}
    sums = {}

    def own(name, g):
        return tops[g] if name == "inv" else env[name]

    def emit(name):
        op = ops[name]
        g = op.info.get("group")
        if op.kind == "inv":
            column = jnp.minimum(device, steps - 1) * rows
            diagonal = lax.dynamic_slice_in_dim(factor[0, 0], column, rows, 1)
            got = call(
                functools.partial(invert_kernel, steps), [diagonal, rhs_blocks[0, 0]],
                [square] + [chunk] * groups,
            )
            env[name] = got[0]
            tops.update(enumerate(got[1:]))
        elif op.kind == "prep":
            scratch = [pltpu.VMEM((repeats, rows, rows), f32), pltpu.SemaphoreType.DMA]
            env[name] = call(
                functools.partial(prepare_kernel, steps, op.info["step"]), [factor, env["inv"]],
                [parts, parts], specs=[hbm, vmem], scratch=scratch,
            )
        elif op.kind == "send":
            env[name] = lax.ppermute(own(op.deps[0], g), "blk", op.pairs)
        elif op.kind == "held":
            value = own(op.deps[0], g)
            for other in op.deps[1:]:
                here = functools.reduce(jnp.logical_or, [device == b for _, b in ops[other].pairs])
                value = jnp.where(here, env[other], value)
            env[name] = value
        elif op.kind == "solve":
            ins = [own(op.deps[0], g)]
            for dep in op.deps[1:]:
                ins += env[dep] if ops[dep].kind == "prep" else [env[dep]]
            env[name] = call(functools.partial(solve_kernel, op.info["device"]), ins, [chunk])[0]
        else:
            k, last = op.info["step"], op.info["last"]
            names = [n for n in op.deps[1:] if ops[n].kind != "rest"]
            ins = list(env[op.deps[0]]) + [rest[g]] + [own(n, g) for n in names]
            outs = [below] + ([shape((1, wide), f32)] if last else [])
            scratch = [pltpu.VMEM((rows, wide), jnp.bfloat16)] * 2
            got = call(
                functools.partial(rest_kernel, steps, k, last), ins, outs, scratch=scratch,
                input_output_aliases={3: 0},
            )
            rest[g] = env[name] = got[0]
            if last:
                sums[g] = got[1]

    for name in order:
        emit(name)

    total = jnp.concatenate([sums[g] for g in range(groups)], axis=1)[0]
    send = lambda value, pairs: lax.ppermute(value, "blk", pairs)
    if count & (count - 1) == 0:
        distance = 1
        while distance < count:
            total = total + send(total, [(i, i ^ distance) for i in range(count)])
            distance *= 2
    else:
        total = lax.psum(total, "blk")
    rest_count = (repeats * count - steps) * rows
    rest_rms = jnp.sqrt(total / rest_count + 1e-06)[None, :]

    ins = []
    for g in range(groups):
        ins += [own("inv" if k == 0 else f"early{k}_{g}", g) for k in range(steps)] + [rest[g]]
    solved = call(
        functools.partial(finish_kernel, steps), ins, [shape((repeats, rows, width), f32)],
        out_specs=[hbm], scratch=[pltpu.SemaphoreType.DMA((repeats, groups))],
    )[0]
    return (solved[:, None], rest_rms)


def solution(mesh):
    placed = (P("groups", "blk", None, None), P("groups", "blk", None, "rhs"))
    count = mesh.shape["blk"]

    def whole(factor, rhs_blocks):
        steps = factor.shape[3] // factor.shape[2]
        ops = make_plan(count, steps, GROUPS)
        order = arrange(ops, ORDER)
        mapped = jax.shard_map(
            functools.partial(body, order, ops),
            mesh=mesh,
            in_specs=placed,
            out_specs=(P("groups", "blk", None, "rhs"), P("groups", "rhs")),
            check_vma=False,
        )
        return mapped(factor, rhs_blocks)

    return whole
```
